32 devices in a mesh: groups: 2 (over y), row: 8 (over z, x), col: 2 (over core).
Axes of the slice: x: 2, y: 2, z: 4, core: 2. Of those that a mesh axis runs over, the one named last changes fastest.
Arguments:
- concentration: float32 [512, 256, 256], P('groups', 'row', 'col'), parts along dimension 0, may hold values from -6 to 6
- species: int32 [2], P('groups'), parts along dimension 0, may hold values from 0 to 63
- reaction_rates: float32 [64], replicated, may hold values from 0.2 to 0.8
- levels: float32 [64], replicated, may hold values from -1 to 1
- sweep_flags: int32 [2, 3], replicated, may hold values from 0 to 1
- explicit_line: float32 [256, 256], replicated, may hold values from -0.5 to 1.2
- inverse_line: float32 [256, 256], replicated, may hold values from -0.5 to 1.2
- explicit_depth: float32 [256, 256], replicated, may hold values from -0.5 to 1.2
- inverse_depth: float32 [256, 256], replicated, may hold values from -0.5 to 1.2
Outputs:
- advanced: float32 [512, 256, 256], P('groups', 'row', 'col'), parts along dimension 0
The draws below stay inside these ranges and needn't reach their ends.
There are 2 independent parts, one for each index of `groups`. The reference program is written for one: setup_inputs(seed, part) draws one part's arguments, and reference() takes and returns one part's arrays. A program takes and returns all parts, laid end to end along the dimension named above; an argument that names none is the same for every part. Nothing has to cross between parts.
All inputs are finite; a program needn't handle non-finite values.
Results may differ from the reference program's by a relative error of at most 0.00011.
Values sent between devices are 32-bit elements; how exact they have to be, the bound alone decides.
A program may use at most 64 MiB of HBM per device.

```python
import math
import jax
import jax.numpy as jnp
from jax import lax

NL = 256
NZ = 256
STEPS = 2
SPECIES = 64


def build_operator(key, order_size, lowest, highest):
    key_diagonal, key_spread = jax.random.split(key)
    diagonal_part = jax.random.uniform(key_diagonal, (order_size,), jnp.float32, lowest, highest)
    spread_part = jnp.clip(jax.random.normal(key_spread, (order_size, order_size), jnp.float32), -3.0, 3.0)
    spread_part = spread_part * (0.3 / math.sqrt(order_size))
    return spread_part + jnp.diag(diagonal_part)


def draw_explicit_line(key, part):
    return build_operator(jax.random.fold_in(key, 11), NL, 0.9, 1.1)


def draw_inverse_line(key, part):
    return build_operator(jax.random.fold_in(key, 23), NL, 0.8, 1.0)


def draw_explicit_depth(key, part):
    return build_operator(jax.random.fold_in(key, 37), NZ, 0.9, 1.1)


def draw_inverse_depth(key, part):
    return build_operator(jax.random.fold_in(key, 41), NZ, 0.8, 1.0)


def touch_ends(result, stream_key, low, high):
    longest = result.shape.index(max(result.shape))
    spots = []
    for shift in (0, 1):
        where = [jax.random.randint(jax.random.fold_in(stream_key, axis), (), 0, length) for axis, length in enumerate(result.shape)]
        where[longest] = (where[longest] + shift) % result.shape[longest]
        spots.append(tuple(where))
    return result.at[spots[0]].set(low).at[spots[1]].set(high)


def block_scale(rng, dims, shards, least, high):
    def one(dim, parts):
        heights = jax.random.uniform(jax.random.fold_in(jax.random.fold_in(rng, 6), dim), (parts,), jnp.float32, least / len(shards), high / len(shards))
        return jnp.repeat(jnp.exp(heights), dims[dim] // parts).reshape((-1,) + (1,) * (len(dims) - dim - 1))

    factor_of = one(*shards[0])
    for cut in shards[1:]:
        factor_of = factor_of * one(*cut)
    return factor_of


def noise(key, dims, width, bound, shards=(), held_as=jnp.bfloat16):
    values = jax.random.normal(key, dims, jnp.float32) * width
    if len(shards) > 0:
        values = block_scale(key, dims, shards, -0.22, 0.18) * values
    return jnp.clip(values, min=-bound, max=bound).astype(held_as)


def setup_inputs(seed: int = 0, part: int = 0) -> dict:
    key_list = jax.random.split(jax.random.key(seed), 10)
    own_keys = jax.random.split(jax.random.fold_in(key_list[9], part), 10)
    return {
        "concentration": noise(own_keys[0], (NL, NL, NZ), 1.0, 6.0, ((1, 8), (2, 2)), jnp.float32),
        "species": jax.random.randint(own_keys[1], (1,), 0, SPECIES).astype(jnp.int32),
        "reaction_rates": jnp.clip(jnp.exp(jax.random.uniform(key_list[2], (SPECIES,), jnp.float32, math.log(0.2), math.log(0.8))), 0.2, 0.8),
        "levels": jnp.clip(jax.random.uniform(key_list[3], (SPECIES,), jnp.float32, -1.0, 1.0), -1.0, 1.0),
        "sweep_flags": touch_ends(jax.random.randint(key_list[4], (STEPS, 3), 0, 2), jax.random.fold_in(key_list[4], 1), 0, 1).astype(jnp.int32),
        "explicit_line": draw_explicit_line(jax.random.fold_in(key_list[9], 71), part),
        "inverse_line": draw_inverse_line(jax.random.fold_in(key_list[9], 71), part),
        "explicit_depth": draw_explicit_depth(jax.random.fold_in(key_list[9], 71), part),
        "inverse_depth": draw_inverse_depth(jax.random.fold_in(key_list[9], 71), part),
    }


def apply_line(matrix, field_now, axis_dim):
    if axis_dim == 0:
        return jnp.einsum("ij,jbc->ibc", matrix, field_now, precision=lax.Precision.HIGHEST)
    if axis_dim == 1:
        return jnp.einsum("ij,ajc->aic", matrix, field_now, precision=lax.Precision.HIGHEST)
    return jnp.einsum("ij,abj->abi", matrix, field_now, precision=lax.Precision.HIGHEST)


def oriented(matrix, reflect):
    return jnp.where(reflect == 1, matrix[::-1, ::-1], matrix)


def reference(concentration, species, reaction_rates, levels, sweep_flags, explicit_line, inverse_line, explicit_depth, inverse_depth):
    picker = (jnp.arange(reaction_rates.shape[0], dtype=jnp.int32) == species[0]).astype(jnp.float32)
    kinetic_rate = jnp.sum(reaction_rates * picker)
    equilibrium = jnp.sum(levels * picker)
    field_now = concentration
    for step_index in range(STEPS):
        order = [0, 1, 2] if step_index % 2 == 0 else [2, 1, 0]
        for axis_dim in order:
            if axis_dim < 2:
                explicit_now, inverse_now = explicit_line, inverse_line
            else:
                explicit_now, inverse_now = explicit_depth, inverse_depth
            reflect = sweep_flags[step_index, axis_dim]
            field_now = field_now - kinetic_rate * jnp.tanh(field_now - equilibrium)
            field_now = apply_line(oriented(explicit_now, reflect), field_now, axis_dim)
            field_now = apply_line(oriented(inverse_now, reflect), field_now, axis_dim)
    return field_now
```

```python
import functools

import jax
import jax.numpy as jnp
from jax import lax
from jax.experimental import pallas as pl
from jax.experimental.pallas import tpu as pltpu
from jax.sharding import PartitionSpec as P

MESH = pl.DeviceIdType.MESH
LANES = 128


def react(v, rate, level):
    return v - rate * jnp.tanh(v - level)


def split(v):
    hi = v.astype(jnp.bfloat16)
    lo = (v - hi.astype(jnp.float32)).astype(jnp.bfloat16)
    return hi, lo


def dot3(a, b):
    (ah, al), (bh, bl) = a, b
    dot = functools.partial(jnp.dot, preferred_element_type=jnp.float32)
    return dot(ah, bh) + (dot(ah, bl) + dot(al, bh))


def load_columns(ref, r, width):
    lines, rows, lanes = ref.shape
    if rows % 8 == 0:
        flat = ref.reshape(lines * rows, lanes)
        parts = [flat[pl.ds(r + i, lines, stride=rows), :] for i in range(width)]
    else:
        parts = [ref[:, r + i, :] for i in range(width)]
    return jnp.concatenate(parts, axis=1)


def store_columns(ref, r, width, value):
    lines, rows, lanes = ref.shape
    for i in range(width):
        part = value[:, i * lanes : (i + 1) * lanes]
        if rows % 8 == 0:
            flat = ref.reshape(lines * rows, lanes)
            flat[pl.ds(r + i, lines, stride=rows), :] = part
        else:
            ref[:, r + i, :] = part


def middle_kernel(
    n, L, R, C, G,
    scal_ref, mats_ref, x_hbm, f_hbm,
    x, y, z, w, v, h, t, u, mh, ml,
    x_sem, own1, own2, send1, recv1, send2, recv2, a_send, a_recv, b_send, b_recv,
):
    me = lax.axis_index("row")
    q = lax.axis_index("col")
    rate, level = scal_ref[0], scal_ref[1]
    per = L // C
    pair = 2 if per % 2 == 0 else 1
    group = R // G

    for g in range(G):
        rows = pl.ds(g * group, group)
        pltpu.make_async_copy(x_hbm.at[:, rows], x.at[:, rows], x_sem.at[g]).start()

    barrier = pltpu.get_barrier_semaphore()

    def greet(j, carry):
        pl.semaphore_signal(
            barrier, inc=1, device_id={"row": lax.rem(me + j, n)}, device_id_type=MESH
        )
        return carry

    lax.fori_loop(1, n, greet, 0)
    pl.semaphore_signal(barrier, inc=1, device_id={"col": 1 - q}, device_id_type=MESH)

    for m in range(mats_ref.shape[0]):
        hi, lo = split(mats_ref[m])
        mh[m] = hi
        ml[m] = lo

    first = (mh[0], ml[0])
    cols = 2 if group % 2 == 0 else 1
    for g in range(G):
        rows = pl.ds(g * group, group)
        pltpu.make_async_copy(x_hbm.at[:, rows], x.at[:, rows], x_sem.at[g]).wait()

        def sweep(s, carry, g=g):
            r = g * group + s * cols
            k = split(react(load_columns(x, r, cols), rate, level))
            store_columns(y, r, cols, dot3(first, k))
            return carry

        if R % 8 == 0:
            lax.fori_loop(0, group // cols, sweep, 0)
        else:
            for s in range(group // cols):
                sweep(s, 0)

    pl.semaphore_wait(barrier, n)

    def send_chunk(c, carry):
        def send_to(j, inner):
            d = lax.rem(me + j, n)
            pltpu.make_async_remote_copy(
                src_ref=y.at[pl.ds(d * L + c * per, per)],
                dst_ref=z.at[pl.ds(c * per, per), me],
                send_sem=send1,
                recv_sem=recv1.at[c],
                device_id={"row": d},
                device_id_type=MESH,
            ).start()
            return inner

        lax.fori_loop(1, n, send_to, 0)
        pltpu.make_async_copy(
            y.at[pl.ds(me * L + c * per, per)], z.at[pl.ds(c * per, per), me], own1.at[c]
        ).start()
        return carry

    lax.fori_loop(0, C, send_chunk, 0)

    half = n * R // 2
    mine = pl.ds(pl.multiple_of(q * half, half), half)
    theirs = pl.ds(pl.multiple_of((1 - q) * half, half), half)
    lanes_mine = pl.ds(pl.multiple_of(q * LANES, LANES), LANES)
    lanes_theirs = pl.ds(pl.multiple_of((1 - q) * LANES, LANES), LANES)
    peer = {"col": 1 - q}

    def chunk(c, carry):
        at = pl.ds(c * per, per)
        pltpu.make_async_copy(z.at[at, pl.ds(0, n - 1)], z.at[at, pl.ds(0, n - 1)], recv1.at[c]).wait()
        pltpu.make_async_copy(
            y.at[pl.ds(me * L + c * per, per)], z.at[at, me], own1.at[c]
        ).wait()

        line = tuple(jnp.concatenate([m[1, mine, :], m[1, theirs, :]], axis=0) for m in (mh, ml))
        for s in range(0, per, pair):
            i = c * per + s
            k = jnp.concatenate([z[i + e].reshape(n * R, LANES) for e in range(pair)], axis=1)
            out = dot3(line, split(react(k, rate, level)))
            for e in range(pair):
                part = out[:, e * LANES : (e + 1) * LANES]
                v[i + e, :, lanes_mine] = part[:half]
                w[i + e] = part[half:]
        to_peer = pltpu.make_async_remote_copy(
            src_ref=w.at[at],
            dst_ref=v.at[at, :, lanes_mine],
            send_sem=a_send.at[c],
            recv_sem=a_recv.at[c],
            device_id=peer,
            device_id_type=MESH,
        )
        to_peer.start()
        to_peer.wait()

        k = v[at].reshape(per * half, 2 * LANES)
        k = dot3(split(react(k, rate, level)), (mh[2], ml[2]))
        depth = tuple(
            jnp.concatenate([m[3, :, lanes_mine], m[3, :, lanes_theirs]], axis=1) for m in (mh, ml)
        )
        k = dot3(split(react(k, rate, level)), depth)
        t[at, mine, :] = k[:, :LANES].reshape(per, half, LANES)
        h[at] = k[:, LANES:].reshape(per, half, LANES)
        to_peer = pltpu.make_async_remote_copy(
            src_ref=h.at[at],
            dst_ref=t.at[at, mine, :],
            send_sem=b_send.at[c],
            recv_sem=b_recv.at[c],
            device_id=peer,
            device_id_type=MESH,
        )
        to_peer.start()
        to_peer.wait()

        line = (mh[4], ml[4])
        for s in range(0, per, pair):
            i = c * per + s
            k = jnp.concatenate([t[i + e] for e in range(pair)], axis=1)
            out = dot3(line, split(react(k, rate, level)))
            for e in range(pair):
                u[i + e] = out[:, e * LANES : (e + 1) * LANES].reshape(n, R, LANES)

        def send_to(j, inner):
            d = lax.rem(me + j, n)
            pltpu.make_async_remote_copy(
                src_ref=u.at[at, d],
                dst_ref=f_hbm.at[pl.ds(me * L + c * per, per)],
                send_sem=send2,
                recv_sem=recv2,
                device_id={"row": d},
                device_id_type=MESH,
            ).start()
            return inner

        lax.fori_loop(1, n, send_to, 0)
        pltpu.make_async_copy(
            u.at[at, me], f_hbm.at[pl.ds(me * L + c * per, per)], own2
        ).start()
        return carry

    lax.fori_loop(0, C, chunk, 0)

    away = y.at[pl.ds(0, (n - 1) * L)]
    pltpu.make_async_copy(away, away, send1).wait()
    pltpu.make_async_copy(away, away, send2).wait()
    own = y.at[pl.ds(0, L)]
    pltpu.make_async_copy(own, own, own2).wait()
    pltpu.make_async_copy(away, away, recv2).wait()


def last_kernel(scal_ref, mat_ref, f_ref, o_ref):
    rate, level = scal_ref[0], scal_ref[1]
    R = f_ref.shape[1]
    matrix = split(mat_ref[...])
    cols = 2 if R % 2 == 0 else 1

    def sweep(s, carry):
        k = split(react(load_columns(f_ref, s * cols, cols), rate, level))
        store_columns(o_ref, s * cols, cols, dot3(matrix, k))
        return carry

    if R % 8 == 0:
        lax.fori_loop(0, R // cols, sweep, 0)
    else:
        for s in range(R // cols):
            sweep(s, 0)


def on_device(
    n,
    concentration,
    species,
    reaction_rates,
    levels,
    sweep_flags,
    explicit_line,
    inverse_line,
    explicit_depth,
    inverse_depth,
):
    picker = (jnp.arange(reaction_rates.shape[0], dtype=jnp.int32) == species[0]).astype(
        jnp.float32
    )
    scalars = jnp.stack([jnp.sum(reaction_rates * picker), jnp.sum(levels * picker)])
    line = jnp.dot(inverse_line, explicit_line, precision=lax.Precision.HIGHEST)
    depth = jnp.dot(
        explicit_depth.T, inverse_depth.T, precision=lax.Precision.HIGHEST
    )
    order = [(0, 0), (0, 1), (0, 2), (1, 2), (1, 1), (1, 0)]
    stack = jnp.stack([depth if d == 2 else line for _, d in order])
    flags = jnp.stack([sweep_flags[s, d] for s, d in order])
    mats = jnp.where(flags[:, None, None] == 1, stack[:, ::-1, ::-1], stack)

    lines, R, lanes = concentration.shape
    L = lines // n
    C = max(1, L // 4)
    G = max(1, R // 8)
    f32 = jnp.float32
    any_spec = pl.BlockSpec(memory_space=pl.ANY)
    smem = pl.BlockSpec(memory_space=pltpu.SMEM)
    dma = pltpu.SemaphoreType.DMA
    half = n * R // 2
    field = pl.pallas_call(
        functools.partial(middle_kernel, n, L, R, C, G),
        out_shape=jax.ShapeDtypeStruct(concentration.shape, f32),
        in_specs=[smem, pl.BlockSpec(memory_space=pltpu.VMEM), any_spec],
        out_specs=any_spec,
        scratch_shapes=[
            pltpu.VMEM((lines, R, lanes), f32),
            pltpu.VMEM((lines, R, lanes), f32),
            pltpu.VMEM((L, n, R, lanes), f32),
            pltpu.VMEM((L, half, lanes), f32),
            pltpu.VMEM((L, half, 2 * lanes), f32),
            pltpu.VMEM((L, half, lanes), f32),
            pltpu.VMEM((L, 2 * half, lanes), f32),
            pltpu.VMEM((L, n, R, lanes), f32),
            pltpu.VMEM(mats.shape, jnp.bfloat16),
            pltpu.VMEM(mats.shape, jnp.bfloat16),
            dma((G,)),
            dma((C,)),
            dma,
            dma,
            dma((C,)),
            dma,
            dma,
            dma((C,)),
            dma((C,)),
            dma((C,)),
            dma((C,)),
        ],
        compiler_params=pltpu.CompilerParams(
            collective_id=0, has_side_effects=True, vmem_limit_bytes=56 << 20
        ),
    )(scalars, mats, concentration)

    rows = R // G
    return pl.pallas_call(
        last_kernel,
        grid=(G,),
        out_shape=jax.ShapeDtypeStruct(concentration.shape, f32),
        in_specs=[
            smem,
            pl.BlockSpec((lines, lines), lambda g: (0, 0)),
            pl.BlockSpec((lines, rows, lanes), lambda g: (0, g, 0)),
        ],
        out_specs=pl.BlockSpec((lines, rows, lanes), lambda g: (0, g, 0)),
        compiler_params=pltpu.CompilerParams(vmem_limit_bytes=32 << 20),
    )(scalars, mats[5], field)


def solution(mesh):
    in_specs = (P("groups", "row", "col"), P("groups"), P(), P(), P(), P(), P(), P(), P())
    out_specs = P("groups", "row", "col")
    return jax.shard_map(
        functools.partial(on_device, mesh.shape["row"]),
        mesh=mesh, in_specs=in_specs, out_specs=out_specs, check_vma=False,
    )
```

```python
import functools

import jax
import jax.numpy as jnp
import numpy as np
from jax import lax
from jax.experimental import pallas as pl
from jax.experimental.pallas import tpu as pltpu
from jax.sharding import PartitionSpec as P

MESH = pl.DeviceIdType.MESH
LANES = 128


def react(v, rate, level):
    return v - rate * jnp.tanh(v - level)


def split(v):
    hi = v.astype(jnp.bfloat16)
    lo = (v - hi.astype(jnp.float32)).astype(jnp.bfloat16)
    return hi, lo


def dot3(a, b):
    (ah, al), (bh, bl) = a, b
    dot = functools.partial(jnp.dot, preferred_element_type=jnp.float32)
    return dot(ah, bh) + (dot(ah, bl) + dot(al, bh))


def load_columns(ref, r, width, start, lines):
    rows, lanes = ref.shape[1:]
    if rows % 8 == 0:
        flat = ref.reshape(ref.shape[0] * rows, lanes)
        parts = [flat[pl.ds(start * rows + r + i, lines, stride=rows), :] for i in range(width)]
    else:
        parts = [ref[start : start + lines, r + i, :] for i in range(width)]
    return jnp.concatenate(parts, axis=1)


def store_columns(ref, r, width, value):
    lines, rows, lanes = ref.shape
    for i in range(width):
        part = value[:, i * lanes : (i + 1) * lanes]
        if rows % 8 == 0:
            flat = ref.reshape(lines * rows, lanes)
            flat[pl.ds(r + i, lines, stride=rows), :] = part
        else:
            ref[:, r + i, :] = part


def move(source, target):
    return jnp.dot(source, target, preferred_element_type=jnp.float32).astype(jnp.bfloat16)


def orientations(matrix):
    size = matrix.shape[0]
    i = lax.broadcasted_iota(jnp.int32, (size, size), 0)
    j = lax.broadcasted_iota(jnp.int32, (size, size), 1)
    exchange = jnp.where(i + j == size - 1, 1.0, 0.0).astype(jnp.bfloat16)
    halves = split(matrix)
    return halves, tuple(move(move(exchange, m), exchange) for m in halves)


def choose(flag, plain, turned):
    where = jnp.full(plain[0].shape, flag, jnp.int32) == 1
    return tuple(
        jnp.where(where, b.astype(jnp.float32), a.astype(jnp.float32)).astype(jnp.bfloat16)
        for a, b in zip(plain, turned)
    )


def fold(inverse, explicit, transposed):
    if transposed:
        inverse, explicit = explicit.T, inverse.T
    return jnp.dot(
        inverse,
        explicit,
        precision=lax.Precision.HIGHEST,
        preferred_element_type=jnp.float32,
    )


def loop_columns(count, ref, body):
    if ref.shape[1] % 8 == 0:
        lax.fori_loop(0, count, body, 0)
    else:
        for s in range(count):
            body(s, 0)


def kernel(
    n, L, R, C, G,
    species, rates, levels, flags, e_line, p_line, e_depth, p_depth, pick_a, pick_b,
    x_hbm, o_hbm,
    x, y, z, w, v, h, t, u, f, mh, ml, ma, mb,
    x_sem, own1, own2, send1, recv1, send2, recv2, a_send, a_recv, b_send, b_recv, o_sem,
):
    me = lax.axis_index("row")
    q = lax.axis_index("col")
    per = L // C
    pair = 2 if per % 2 == 0 else 1
    group = R // G

    for g in range(G):
        rows = pl.ds(g * group, group)
        pltpu.make_async_copy(x_hbm.at[:, rows], x.at[:, rows], x_sem.at[g]).start()

    barrier = pltpu.get_barrier_semaphore()

    def greet(j, carry):
        pl.semaphore_signal(
            barrier, inc=1, device_id={"row": lax.rem(me + j, n)}, device_id_type=MESH
        )
        return carry

    lax.fori_loop(1, n, greet, 0)
    pl.semaphore_signal(barrier, inc=1, device_id={"col": 1 - q}, device_id_type=MESH)

    kind = species[0]
    rate, level = rates[kind], levels[kind]

    def keep(slot, flag, plain, turned):
        mh[slot], ml[slot] = choose(flag, plain, turned)

    lines = orientations(fold(p_line[...], e_line[...], False))
    keep(0, flags[0, 0], *lines)
    keep(1, flags[0, 1], *lines)
    keep(4, flags[1, 1], *lines)
    final = choose(flags[1, 0], *lines)
    if C > 1:
        ma[...] = (
            jnp.dot(final[0], pick_a[0], preferred_element_type=jnp.float32)
            + jnp.dot(final[1], pick_a[1], preferred_element_type=jnp.float32)
        ).astype(jnp.bfloat16)
    mb[...] = (
        jnp.dot(final[0], pick_b[0], preferred_element_type=jnp.float32)
        + jnp.dot(final[1], pick_b[1], preferred_element_type=jnp.float32)
    ).astype(jnp.bfloat16)

    def send_rows(c, rows):
        def send_to(j, inner):
            d = lax.rem(me + j, n)
            pltpu.make_async_remote_copy(
                src_ref=y.at[pl.ds(d * L + c * per, per), rows],
                dst_ref=z.at[pl.ds(c * per, per), me, rows],
                send_sem=send1,
                recv_sem=recv1.at[c],
                device_id={"row": d},
                device_id_type=MESH,
            ).start()
            return inner

        lax.fori_loop(1, n, send_to, 0)

    first = (mh[0], ml[0])
    cols = 2 if group % 2 == 0 else 1
    for g in range(G):
        rows = pl.ds(g * group, group)
        pltpu.make_async_copy(x_hbm.at[:, rows], x.at[:, rows], x_sem.at[g]).wait()

        def sweep(s, carry, g=g):
            r = g * group + s * cols
            k = split(react(load_columns(x, r, cols, 0, n * L), rate, level))
            store_columns(y, r, cols, dot3(first, k))
            return carry

        loop_columns(group // cols, x, sweep)
        if g == 0:
            pl.semaphore_wait(barrier, n)
        send_rows(0, rows)

    def own_copy(c):
        return pltpu.make_async_copy(
            y.at[pl.ds(me * L + c * per, per)], z.at[pl.ds(c * per, per), me], own1.at[c]
        )

    def send_chunk(c, carry):
        send_rows(c, pl.ds(0, R))
        own_copy(c).start()
        return carry

    own_copy(0).start()
    lax.fori_loop(1, C, send_chunk, 0)

    depths = orientations(fold(p_depth[...], e_depth[...], True))
    keep(2, flags[0, 2], *depths)
    keep(3, flags[1, 2], *depths)

    half = n * R // 2
    mine = pl.ds(pl.multiple_of(q * half, half), half)
    theirs = pl.ds(pl.multiple_of((1 - q) * half, half), half)
    lanes_mine = pl.ds(pl.multiple_of(q * LANES, LANES), LANES)
    lanes_theirs = pl.ds(pl.multiple_of((1 - q) * LANES, LANES), LANES)
    peer = {"col": 1 - q}

    def back(c):
        return f.at[pl.ds(c * (n * per) + me * per, per)]

    def chunk(c, carry):
        at = pl.ds(c * per, per)
        arrived = z.at[at, pl.ds(0, n - 1)]
        pltpu.make_async_copy(arrived, arrived, recv1.at[c]).wait()
        own_copy(c).wait()

        line = tuple(jnp.concatenate([m[1, mine, :], m[1, theirs, :]], axis=0) for m in (mh, ml))
        for s in range(0, per, pair):
            i = c * per + s
            k = jnp.concatenate([z[i + e].reshape(n * R, LANES) for e in range(pair)], axis=1)
            out = dot3(line, split(react(k, rate, level)))
            for e in range(pair):
                part = out[:, e * LANES : (e + 1) * LANES]
                v[i + e, :, lanes_mine] = part[:half]
                w[i + e] = part[half:]
        to_peer = pltpu.make_async_remote_copy(
            src_ref=w.at[at],
            dst_ref=v.at[at, :, lanes_mine],
            send_sem=a_send.at[c],
            recv_sem=a_recv.at[c],
            device_id=peer,
            device_id_type=MESH,
        )
        to_peer.start()
        to_peer.wait()

        k = v[at].reshape(per * half, 2 * LANES)
        k = dot3(split(react(k, rate, level)), (mh[2], ml[2]))
        depth = tuple(
            jnp.concatenate([m[3, :, lanes_mine], m[3, :, lanes_theirs]], axis=1) for m in (mh, ml)
        )
        k = dot3(split(react(k, rate, level)), depth)
        t[at, mine, :] = k[:, :LANES].reshape(per, half, LANES)
        h[at] = k[:, LANES:].reshape(per, half, LANES)
        to_peer = pltpu.make_async_remote_copy(
            src_ref=h.at[at],
            dst_ref=t.at[at, mine, :],
            send_sem=b_send.at[c],
            recv_sem=b_recv.at[c],
            device_id=peer,
            device_id_type=MESH,
        )
        to_peer.start()
        to_peer.wait()

        line = (mh[4], ml[4])
        for s in range(0, per, pair):
            i = c * per + s
            k = jnp.concatenate([t[i + e] for e in range(pair)], axis=1)
            out = dot3(line, split(react(k, rate, level)))
            for e in range(pair):
                u[i + e] = out[:, e * LANES : (e + 1) * LANES].reshape(n, R, LANES)

        def send_to(j, inner):
            d = lax.rem(me + j, n)
            pltpu.make_async_remote_copy(
                src_ref=u.at[at, d],
                dst_ref=back(c),
                send_sem=send2,
                recv_sem=recv2.at[c],
                device_id={"row": d},
                device_id_type=MESH,
            ).start()
            return inner

        lax.fori_loop(1, n, send_to, 0)
        pltpu.make_async_copy(u.at[at, me], back(c), own2.at[c]).start()
        return carry

    lax.fori_loop(0, C, chunk, 0)

    def wait_back(c, carry):
        arrived = f.at[pl.ds(c * (n * per), (n - 1) * per)]
        pltpu.make_async_copy(arrived, arrived, recv2.at[c]).wait()
        pltpu.make_async_copy(u.at[pl.ds(c * per, per), me], back(c), own2.at[c]).wait()
        return carry

    def terms(matrix, r, start, count):
        hi, lo = split(react(load_columns(f, r, cols, start, count), rate, level))
        k = jnp.concatenate([hi, lo, hi], axis=0)
        return jnp.dot(matrix, k, preferred_element_type=jnp.float32)

    early = (C - 1) * n * per
    if C > 1:
        lax.fori_loop(0, C - 1, wait_back, 0)
        lead = ma[...]

        def begin(s, carry):
            store_columns(x, s * cols, cols, terms(lead, s * cols, 0, early))
            return carry

        loop_columns(R // cols, x, begin)
    wait_back(C - 1, 0)
    rest = mb[...]

    def o_copy(g):
        rows = pl.ds(g * group, group)
        return pltpu.make_async_copy(x.at[:, rows], o_hbm.at[:, rows], o_sem.at[g])

    for g in range(G):

        def finish(s, carry, g=g):
            r = g * group + s * cols
            total = terms(rest, r, early, n * per)
            if C > 1:
                total += load_columns(x, r, cols, 0, n * L)
            store_columns(x, r, cols, total)
            return carry

        loop_columns(group // cols, x, finish)
        o_copy(g).start()

    away = y.at[pl.ds(0, (n - 1) * L)]
    pltpu.make_async_copy(away, away, send1).wait()
    pltpu.make_async_copy(away, away, send2).wait()
    for g in range(G):
        o_copy(g).wait()


def on_device(
    n,
    concentration,
    species,
    reaction_rates,
    levels,
    sweep_flags,
    explicit_line,
    inverse_line,
    explicit_depth,
    inverse_depth,
):
    lines, R, lanes = concentration.shape
    L = lines // n
    C = max(1, L // 4)
    G = max(1, R // 8)
    per = L // C
    half = n * R // 2
    f32, bf16 = jnp.float32, jnp.bfloat16

    c, source, e = np.meshgrid(np.arange(C), np.arange(n), np.arange(per), indexing="ij")
    held = (source * L + c * per + e).reshape(-1)
    early = (C - 1) * n * per
    picks = []
    for part in (held[:early], held[early:]):
        pick = np.zeros((lines, len(part)), np.float32)
        pick[part, np.arange(len(part))] = 1
        none = np.zeros_like(pick)
        picks.append(
            np.stack([np.concatenate(m, 1) for m in ((pick, pick, none), (none, none, pick))])
        )
    if C == 1:
        picks[0] = picks[1]
    pick_a, pick_b = (jnp.asarray(p.astype(bf16)) for p in picks)

    any_spec = pl.BlockSpec(memory_space=pl.ANY)
    smem = pl.BlockSpec(memory_space=pltpu.SMEM)
    vmem = pl.BlockSpec(memory_space=pltpu.VMEM)
    dma = pltpu.SemaphoreType.DMA
    return pl.pallas_call(
        functools.partial(kernel, n, L, R, C, G),
        out_shape=jax.ShapeDtypeStruct(concentration.shape, f32),
        in_specs=[smem] * 4 + [vmem] * 6 + [any_spec],
        out_specs=any_spec,
        scratch_shapes=[
            pltpu.VMEM((lines, R, lanes), f32),
            pltpu.VMEM((lines, R, lanes), f32),
            pltpu.VMEM((L, n, R, lanes), f32),
            pltpu.VMEM((L, half, lanes), f32),
            pltpu.VMEM((L, half, 2 * lanes), f32),
            pltpu.VMEM((L, half, lanes), f32),
            pltpu.VMEM((L, 2 * half, lanes), f32),
            pltpu.VMEM((L, n, R, lanes), f32),
            pltpu.VMEM((lines, R, lanes), f32),
            pltpu.VMEM((5, lines, lines), bf16),
            pltpu.VMEM((5, lines, lines), bf16),
            pltpu.VMEM((lines, pick_a.shape[2]), bf16),
            pltpu.VMEM((lines, pick_b.shape[2]), bf16),
            dma((G,)),
            dma((C,)),
            dma((C,)),
            dma,
            dma((C,)),
            dma,
            dma((C,)),
            dma((C,)),
            dma((C,)),
            dma((C,)),
            dma((C,)),
            dma((G,)),
        ],
        compiler_params=pltpu.CompilerParams(
            collective_id=0, has_side_effects=True, vmem_limit_bytes=58 << 20
        ),
    )(
        species, reaction_rates, levels, sweep_flags,
        explicit_line, inverse_line, explicit_depth, inverse_depth,
        pick_a, pick_b, concentration,
    )


def solution(mesh):
    in_specs = (P("groups", "row", "col"), P("groups"), P(), P(), P(), P(), P(), P(), P())
    out_specs = P("groups", "row", "col")
    return jax.shard_map(
        functools.partial(on_device, mesh.shape["row"]),
        mesh=mesh, in_specs=in_specs, out_specs=out_specs, check_vma=False,
    )
```

```python
import functools

import jax
import jax.numpy as jnp
import numpy as np
from jax import lax
from jax.experimental import pallas as pl
from jax.experimental.pallas import tpu as pltpu
from jax.sharding import PartitionSpec as P

MESH = pl.DeviceIdType.MESH
LANES = 128


def react(v, rate, level):
    return v - rate * jnp.tanh(v - level)


def split(v):
    hi = v.astype(jnp.bfloat16)
    lo = (v - hi.astype(jnp.float32)).astype(jnp.bfloat16)
    return hi, lo


def dot3(a, b):
    (ah, al), (bh, bl) = a, b
    dot = functools.partial(jnp.dot, preferred_element_type=jnp.float32)
    return dot(ah, bh) + (dot(ah, bl) + dot(al, bh))


def load_columns(ref, r, width, start, lines):
    rows, lanes = ref.shape[1:]
    if rows % 8 == 0:
        flat = ref.reshape(ref.shape[0] * rows, lanes)
        parts = [flat[pl.ds(start * rows + r + i, lines, stride=rows), :] for i in range(width)]
    else:
        parts = [ref[start : start + lines, r + i, :] for i in range(width)]
    return jnp.concatenate(parts, axis=1)


def store_columns(ref, r, width, value):
    lines, rows, lanes = ref.shape
    for i in range(width):
        part = value[:, i * lanes : (i + 1) * lanes]
        if rows % 8 == 0:
            flat = ref.reshape(lines * rows, lanes)
            flat[pl.ds(r + i, lines, stride=rows), :] = part
        else:
            ref[:, r + i, :] = part


def move(source, target):
    return jnp.dot(source, target, preferred_element_type=jnp.float32).astype(jnp.bfloat16)


def orientations(matrix):
    size = matrix.shape[0]
    i = lax.broadcasted_iota(jnp.int32, (size, size), 0)
    j = lax.broadcasted_iota(jnp.int32, (size, size), 1)
    exchange = jnp.where(i + j == size - 1, 1.0, 0.0).astype(jnp.bfloat16)
    halves = split(matrix)
    return halves, tuple(move(move(exchange, m), exchange) for m in halves)


def choose(flag, plain, turned):
    where = jnp.full(plain[0].shape, flag, jnp.int32) == 1
    return tuple(
        jnp.where(where, b.astype(jnp.float32), a.astype(jnp.float32)).astype(jnp.bfloat16)
        for a, b in zip(plain, turned)
    )


def fold(inverse, explicit, transposed):
    if transposed:
        inverse, explicit = explicit.T, inverse.T
    return jnp.dot(
        inverse,
        explicit,
        precision=lax.Precision.HIGHEST,
        preferred_element_type=jnp.float32,
    )


def loop_columns(count, ref, body):
    if ref.shape[1] % 8 == 0:
        lax.fori_loop(0, count, body, 0)
    else:
        for s in range(count):
            body(s, 0)


def kernel(
    n, L, R, C, G,
    species, rates, levels, flags, e_line, p_line, late_0, late_1, late_2, late_3,
    x_hbm, o_hbm, last, mb,
    x, y, z, w, v, h, t, u, f, mh, ml, ma, e_depth, p_depth, pick_a, pick_b,
    x_sem, own1, own2, send1, recv1, send2, recv2, a_send, a_recv, b_send, b_recv, o_sem, late_sem,
):
    me = lax.axis_index("row")
    q = lax.axis_index("col")
    per = L // C
    pair = 2 if per % 2 == 0 else 1
    group = R // G

    for g in range(G):
        rows = pl.ds(g * group, group)
        pltpu.make_async_copy(x_hbm.at[:, rows], x.at[:, rows], x_sem.at[g]).start()

    late = [
        pltpu.make_async_copy(source, target, late_sem.at[i])
        for i, (source, target) in enumerate(
            zip((late_0, late_1, late_2, late_3), (e_depth, p_depth, pick_a, pick_b))
        )
    ]
    for copy in late:
        copy.start()

    barrier = pltpu.get_barrier_semaphore()

    def greet(j, carry):
        pl.semaphore_signal(
            barrier, inc=1, device_id={"row": lax.rem(me + j, n)}, device_id_type=MESH
        )
        return carry

    lax.fori_loop(1, n, greet, 0)
    pl.semaphore_signal(barrier, inc=1, device_id={"col": 1 - q}, device_id_type=MESH)

    kind = species[0]
    rate, level = rates[kind], levels[kind]

    def keep(slot, flag, plain, turned):
        mh[slot], ml[slot] = choose(flag, plain, turned)

    lines = orientations(fold(p_line[...], e_line[...], False))
    keep(0, flags[0, 0], *lines)

    def send_rows(c, rows):
        def send_to(j, inner):
            d = lax.rem(me + j, n)
            pltpu.make_async_remote_copy(
                src_ref=y.at[pl.ds(d * L + c * per, per), rows],
                dst_ref=z.at[pl.ds(c * per, per), me, rows],
                send_sem=send1,
                recv_sem=recv1.at[c],
                device_id={"row": d},
                device_id_type=MESH,
            ).start()
            return inner

        lax.fori_loop(1, n, send_to, 0)

    first = (mh[0], ml[0])
    cols = 2 if group % 2 == 0 else 1
    for g in range(G):
        rows = pl.ds(g * group, group)
        pltpu.make_async_copy(x_hbm.at[:, rows], x.at[:, rows], x_sem.at[g]).wait()

        def sweep(s, carry, g=g):
            r = g * group + s * cols
            k = split(react(load_columns(x, r, cols, 0, n * L), rate, level))
            store_columns(y, r, cols, dot3(first, k))
            return carry

        loop_columns(group // cols, x, sweep)
        if g == 0:
            pl.semaphore_wait(barrier, n)
            send_rows(0, rows)
    if G > 1:
        send_rows(0, pl.ds(group, R - group))

    def own_copy(c):
        return pltpu.make_async_copy(
            y.at[pl.ds(me * L + c * per, per)], z.at[pl.ds(c * per, per), me], own1.at[c]
        )

    def send_chunk(c, carry):
        send_rows(c, pl.ds(0, R))
        own_copy(c).start()
        return carry

    own_copy(0).start()
    lax.fori_loop(1, C, send_chunk, 0)

    for copy in late:
        copy.wait()
    keep(1, flags[0, 1], *lines)
    keep(4, flags[1, 1], *lines)
    final = choose(flags[1, 0], *lines)
    ma[...] = (
        jnp.dot(final[0], pick_a[0], preferred_element_type=jnp.float32)
        + jnp.dot(final[1], pick_a[1], preferred_element_type=jnp.float32)
    ).astype(jnp.bfloat16)
    mb[...] = (
        jnp.dot(final[0], pick_b[0], preferred_element_type=jnp.float32)
        + jnp.dot(final[1], pick_b[1], preferred_element_type=jnp.float32)
    ).astype(jnp.bfloat16)
    depths = orientations(fold(p_depth[...], e_depth[...], True))
    keep(2, flags[0, 2], *depths)
    keep(3, flags[1, 2], *depths)

    half = n * R // 2
    mine = pl.ds(pl.multiple_of(q * half, half), half)
    theirs = pl.ds(pl.multiple_of((1 - q) * half, half), half)
    lanes_mine = pl.ds(pl.multiple_of(q * LANES, LANES), LANES)
    lanes_theirs = pl.ds(pl.multiple_of((1 - q) * LANES, LANES), LANES)
    peer = {"col": 1 - q}

    def back(c):
        return f.at[pl.ds(c * (n * per) + me * per, per)]

    back_last = last.at[pl.ds(me * per, per)]

    def chunk(c, carry):
        at = pl.ds(c * per, per)
        arrived = z.at[at, pl.ds(0, n - 1)]
        pltpu.make_async_copy(arrived, arrived, recv1.at[c]).wait()
        own_copy(c).wait()

        line = tuple(jnp.concatenate([m[1, mine, :], m[1, theirs, :]], axis=0) for m in (mh, ml))
        for s in range(0, per, pair):
            i = c * per + s
            k = jnp.concatenate([z[i + e].reshape(n * R, LANES) for e in range(pair)], axis=1)
            out = dot3(line, split(react(k, rate, level)))
            for e in range(pair):
                part = out[:, e * LANES : (e + 1) * LANES]
                v[i + e, :, lanes_mine] = part[:half]
                w[i + e] = part[half:]
        to_peer = pltpu.make_async_remote_copy(
            src_ref=w.at[at],
            dst_ref=v.at[at, :, lanes_mine],
            send_sem=a_send.at[c],
            recv_sem=a_recv.at[c],
            device_id=peer,
            device_id_type=MESH,
        )
        to_peer.start()
        to_peer.wait()

        k = v[at].reshape(per * half, 2 * LANES)
        k = dot3(split(react(k, rate, level)), (mh[2], ml[2]))
        depth = tuple(
            jnp.concatenate([m[3, :, lanes_mine], m[3, :, lanes_theirs]], axis=1) for m in (mh, ml)
        )
        k = dot3(split(react(k, rate, level)), depth)
        t[at, mine, :] = k[:, :LANES].reshape(per, half, LANES)
        h[at] = k[:, LANES:].reshape(per, half, LANES)
        to_peer = pltpu.make_async_remote_copy(
            src_ref=h.at[at],
            dst_ref=t.at[at, mine, :],
            send_sem=b_send.at[c],
            recv_sem=b_recv.at[c],
            device_id=peer,
            device_id_type=MESH,
        )
        to_peer.start()
        to_peer.wait()

        line = (mh[4], ml[4])
        for s in range(0, per, pair):
            i = c * per + s
            k = jnp.concatenate([t[i + e] for e in range(pair)], axis=1)
            out = dot3(line, split(react(k, rate, level)))
            for e in range(pair):
                u[i + e] = out[:, e * LANES : (e + 1) * LANES].reshape(n, R, LANES)

        def send_back(target):
            def send_to(j, inner):
                d = lax.rem(me + j, n)
                pltpu.make_async_remote_copy(
                    src_ref=u.at[at, d],
                    dst_ref=target,
                    send_sem=send2,
                    recv_sem=recv2.at[c],
                    device_id={"row": d},
                    device_id_type=MESH,
                ).start()
                return inner

            lax.fori_loop(1, n, send_to, 0)
            pltpu.make_async_copy(u.at[at, me], target, own2.at[c]).start()

        @pl.when(c < C - 1)
        def _():
            send_back(back(c))

        @pl.when(c == C - 1)
        def _():
            send_back(back_last)

        return carry

    lax.fori_loop(0, C, chunk, 0)

    def wait_back(c, carry):
        arrived = f.at[pl.ds(c * (n * per), (n - 1) * per)]
        pltpu.make_async_copy(arrived, arrived, recv2.at[c]).wait()
        pltpu.make_async_copy(u.at[pl.ds(c * per, per), me], back(c), own2.at[c]).wait()
        return carry

    lax.fori_loop(0, C - 1, wait_back, 0)
    lead = ma[...]

    def o_copy(g):
        rows = pl.ds(g * group, group)
        return pltpu.make_async_copy(x.at[:, rows], o_hbm.at[:, rows], o_sem.at[g])

    for g in range(G):

        def begin(s, carry, g=g):
            r = g * group + s * cols
            store_columns(x, r, cols, terms(lead, f, r, cols, rate, level))
            return carry

        loop_columns(group // cols, x, begin)
        o_copy(g).start()
    for g in range(G):
        o_copy(g).wait()

    away = y.at[pl.ds(0, (n - 1) * L)]
    pltpu.make_async_copy(away, away, send1).wait()
    pltpu.make_async_copy(away, away, send2).wait()
    arrived = last.at[pl.ds(0, (n - 1) * per)]
    pltpu.make_async_copy(arrived, arrived, recv2.at[C - 1]).wait()
    pltpu.make_async_copy(u.at[pl.ds((C - 1) * per, per), me], back_last, own2.at[C - 1]).wait()


def terms(matrix, ref, r, cols, rate, level):
    hi, lo = split(react(load_columns(ref, r, cols, 0, ref.shape[0]), rate, level))
    k = jnp.concatenate([hi, lo, hi], axis=0)
    return jnp.dot(matrix, k, preferred_element_type=jnp.float32)


def last_kernel(species, rates, levels, matrix_ref, last_ref, sum_ref, o_ref):
    kind = species[0]
    rate, level = rates[kind], levels[kind]
    lines, R, lanes = o_ref.shape
    cols = 2 if R % 2 == 0 else 1
    matrix = matrix_ref[...]

    for s in range(R // cols):
        total = load_columns(sum_ref, s * cols, cols, 0, lines)
        total += terms(matrix, last_ref, s * cols, cols, rate, level)
        store_columns(o_ref, s * cols, cols, total)


def on_device(
    n,
    concentration,
    species,
    reaction_rates,
    levels,
    sweep_flags,
    explicit_line,
    inverse_line,
    explicit_depth,
    inverse_depth,
):
    lines, R, lanes = concentration.shape
    L = lines // n
    C = max(2, L // 8)
    G = max(1, R // 8)
    per = L // C
    half = n * R // 2
    f32, bf16 = jnp.float32, jnp.bfloat16

    c, source, e = np.meshgrid(np.arange(C), np.arange(n), np.arange(per), indexing="ij")
    held = (source * L + c * per + e).reshape(-1)
    early = (C - 1) * n * per
    picks = []
    for part in (held[:early], held[early:]):
        pick = np.zeros((lines, len(part)), np.float32)
        pick[part, np.arange(len(part))] = 1
        none = np.zeros_like(pick)
        picks.append(
            np.stack([np.concatenate(m, 1) for m in ((pick, pick, none), (none, none, pick))])
        )
    pick_a, pick_b = (jnp.asarray(p.astype(bf16)) for p in picks)

    any_spec = pl.BlockSpec(memory_space=pl.ANY)
    smem = pl.BlockSpec(memory_space=pltpu.SMEM)
    vmem = pl.BlockSpec(memory_space=pltpu.VMEM)
    dma = pltpu.SemaphoreType.DMA
    whole = jax.ShapeDtypeStruct(concentration.shape, f32)
    partial_sum, last, matrix = pl.pallas_call(
        functools.partial(kernel, n, L, R, C, G),
        out_shape=(
            whole,
            jax.ShapeDtypeStruct((n * per, R, lanes), f32),
            jax.ShapeDtypeStruct((lines, pick_b.shape[2]), bf16),
        ),
        in_specs=[smem] * 4 + [vmem] * 2 + [any_spec] * 5,
        out_specs=(any_spec, any_spec, vmem),
        scratch_shapes=[
            pltpu.VMEM((lines, R, lanes), f32),
            pltpu.VMEM((lines, R, lanes), f32),
            pltpu.VMEM((L, n, R, lanes), f32),
            pltpu.VMEM((L, half, lanes), f32),
            pltpu.VMEM((L, half, 2 * lanes), f32),
            pltpu.VMEM((L, half, lanes), f32),
            pltpu.VMEM((L, 2 * half, lanes), f32),
            pltpu.VMEM((L, n, R, lanes), f32),
            pltpu.VMEM((early, R, lanes), f32),
            pltpu.VMEM((5, lines, lines), bf16),
            pltpu.VMEM((5, lines, lines), bf16),
            pltpu.VMEM((lines, pick_a.shape[2]), bf16),
            pltpu.VMEM(explicit_depth.shape, f32),
            pltpu.VMEM(inverse_depth.shape, f32),
            pltpu.VMEM(pick_a.shape, bf16),
            pltpu.VMEM(pick_b.shape, bf16),
            dma((G,)),
            dma((C,)),
            dma((C,)),
            dma,
            dma((C,)),
            dma,
            dma((C,)),
            dma((C,)),
            dma((C,)),
            dma((C,)),
            dma((C,)),
            dma((G,)),
            dma((4,)),
        ],
        compiler_params=pltpu.CompilerParams(
            collective_id=0, has_side_effects=True, vmem_limit_bytes=58 << 20
        ),
    )(
        species, reaction_rates, levels, sweep_flags,
        explicit_line, inverse_line, explicit_depth, inverse_depth,
        pick_a, pick_b, concentration,
    )

    rows = R // G
    return pl.pallas_call(
        last_kernel,
        grid=(G,),
        out_shape=whole,
        in_specs=[
            smem,
            smem,
            smem,
            pl.BlockSpec(matrix.shape, lambda g: (0, 0)),
            pl.BlockSpec((n * per, rows, lanes), lambda g: (0, g, 0)),
            pl.BlockSpec((lines, rows, lanes), lambda g: (0, g, 0)),
        ],
        out_specs=pl.BlockSpec((lines, rows, lanes), lambda g: (0, g, 0)),
        compiler_params=pltpu.CompilerParams(vmem_limit_bytes=58 << 20),
    )(species, reaction_rates, levels, matrix, last, partial_sum)


def solution(mesh):
    in_specs = (P("groups", "row", "col"), P("groups"), P(), P(), P(), P(), P(), P(), P())
    out_specs = P("groups", "row", "col")
    return jax.shard_map(
        functools.partial(on_device, mesh.shape["row"]),
        mesh=mesh, in_specs=in_specs, out_specs=out_specs, check_vma=False,
    )
```

```python
import functools

import jax
import jax.numpy as jnp
import numpy as np
from jax import lax
from jax.experimental import pallas as pl
from jax.experimental.pallas import tpu as pltpu
from jax.sharding import PartitionSpec as P

MESH = pl.DeviceIdType.MESH
LANES = 128


def react(v, rate, level):
    return v - rate * jnp.tanh(v - level)


def split(v):
    hi = v.astype(jnp.bfloat16)
    lo = (v - hi.astype(jnp.float32)).astype(jnp.bfloat16)
    return hi, lo


def dot3(a, b):
    (ah, al), (bh, bl) = a, b
    dot = functools.partial(jnp.dot, preferred_element_type=jnp.float32)
    return dot(ah, bh) + (dot(ah, bl) + dot(al, bh))


def load_columns(ref, r, width, start, lines):
    rows, lanes = ref.shape[1:]
    if rows % 8 == 0:
        flat = ref.reshape(ref.shape[0] * rows, lanes)
        parts = [flat[pl.ds(start * rows + r + i, lines, stride=rows), :] for i in range(width)]
    else:
        parts = [ref[start : start + lines, r + i, :] for i in range(width)]
    return jnp.concatenate(parts, axis=1)


def store_columns(ref, r, width, value):
    lines, rows, lanes = ref.shape
    for i in range(width):
        part = value[:, i * lanes : (i + 1) * lanes]
        if rows % 8 == 0:
            flat = ref.reshape(lines * rows, lanes)
            flat[pl.ds(r + i, lines, stride=rows), :] = part
        else:
            ref[:, r + i, :] = part


def move(source, target):
    return jnp.dot(source, target, preferred_element_type=jnp.float32).astype(jnp.bfloat16)


def orientations(matrix):
    size = matrix.shape[0]
    i = lax.broadcasted_iota(jnp.int32, (size, size), 0)
    j = lax.broadcasted_iota(jnp.int32, (size, size), 1)
    exchange = jnp.where(i + j == size - 1, 1.0, 0.0).astype(jnp.bfloat16)
    halves = split(matrix)
    return halves, tuple(move(move(exchange, m), exchange) for m in halves)


def choose(flag, plain, turned):
    where = jnp.full(plain[0].shape, flag, jnp.int32) == 1
    return tuple(
        jnp.where(where, b.astype(jnp.float32), a.astype(jnp.float32)).astype(jnp.bfloat16)
        for a, b in zip(plain, turned)
    )


def fold(inverse, explicit, transposed):
    if transposed:
        inverse, explicit = explicit.T, inverse.T
    return jnp.dot(
        inverse,
        explicit,
        precision=lax.Precision.HIGHEST,
        preferred_element_type=jnp.float32,
    )


def loop_columns(count, ref, body):
    if ref.shape[1] % 8 == 0:
        lax.fori_loop(0, count, body, 0)
    else:
        for s in range(count):
            body(s, 0)


def kernel(
    n, L, R, C, G,
    species, rates, levels, flags, e_line, p_line, late_0, late_1, late_2, late_3,
    x_hbm, o_hbm, last, mb,
    x, y, z, w, v, h, t, u, f, mh, ml, ma, e_depth, p_depth, pick_a, pick_b,
    x_sem, own1, own2, send1, recv1, send2, recv2, a_send, a_recv, b_send, b_recv, o_sem, late_sem,
):
    me = lax.axis_index("row")
    q = lax.axis_index("col")
    per = L // C
    pair = 2 if per % 2 == 0 else 1
    group = R // G

    for g in range(G):
        rows = pl.ds(g * group, group)
        pltpu.make_async_copy(x_hbm.at[:, rows], x.at[:, rows], x_sem.at[g]).start()

    late = [
        pltpu.make_async_copy(source, target, late_sem.at[i])
        for i, (source, target) in enumerate(
            zip((late_0, late_1, late_2, late_3), (e_depth, p_depth, pick_a, pick_b))
        )
    ]
    for copy in late:
        copy.start()

    barrier = pltpu.get_barrier_semaphore()

    def greet(j, carry):
        pl.semaphore_signal(
            barrier, inc=1, device_id={"row": lax.rem(me + j, n)}, device_id_type=MESH
        )
        return carry

    lax.fori_loop(1, n, greet, 0)
    pl.semaphore_signal(barrier, inc=1, device_id={"col": 1 - q}, device_id_type=MESH)

    kind = species[0]
    rate, level = rates[kind], levels[kind]

    def keep(slot, flag, plain, turned):
        mh[slot], ml[slot] = choose(flag, plain, turned)

    lines = orientations(fold(p_line[...], e_line[...], False))
    keep(0, flags[0, 0], *lines)

    def send_rows(c, rows):
        def send_to(j, inner):
            d = lax.rem(me + j, n)
            pltpu.make_async_remote_copy(
                src_ref=y.at[pl.ds(d * L + c * per, per), rows],
                dst_ref=z.at[pl.ds(c * per, per), me, rows],
                send_sem=send1,
                recv_sem=recv1.at[c],
                device_id={"row": d},
                device_id_type=MESH,
            ).start()
            return inner

        lax.fori_loop(1, n, send_to, 0)

    first = (mh[0], ml[0])
    cols = 2 if group % 2 == 0 else 1
    for g in range(G):
        rows = pl.ds(g * group, group)
        pltpu.make_async_copy(x_hbm.at[:, rows], x.at[:, rows], x_sem.at[g]).wait()

        def sweep(s, carry, g=g):
            r = g * group + s * cols
            k = split(react(load_columns(x, r, cols, 0, n * L), rate, level))
            store_columns(y, r, cols, dot3(first, k))
            return carry

        loop_columns(group // cols, x, sweep)
        if g == 0:
            pl.semaphore_wait(barrier, n)
            send_rows(0, rows)
    if G > 1:
        send_rows(0, pl.ds(group, R - group))

    def own_copy(c):
        return pltpu.make_async_copy(
            y.at[pl.ds(me * L + c * per, per)], z.at[pl.ds(c * per, per), me], own1.at[c]
        )

    def send_chunk(c, carry):
        send_rows(c, pl.ds(0, R))
        own_copy(c).start()
        return carry

    own_copy(0).start()
    lax.fori_loop(1, C, send_chunk, 0)

    for copy in late:
        copy.wait()
    keep(1, flags[0, 1], *lines)
    keep(4, flags[1, 1], *lines)
    final = choose(flags[1, 0], *lines)
    ma[...] = (
        jnp.dot(final[0], pick_a[0], preferred_element_type=jnp.float32)
        + jnp.dot(final[1], pick_a[1], preferred_element_type=jnp.float32)
    ).astype(jnp.bfloat16)
    mb[...] = (
        jnp.dot(final[0], pick_b[0], preferred_element_type=jnp.float32)
        + jnp.dot(final[1], pick_b[1], preferred_element_type=jnp.float32)
    ).astype(jnp.bfloat16)
    depths = orientations(fold(p_depth[...], e_depth[...], True))
    keep(2, flags[0, 2], *depths)
    keep(3, flags[1, 2], *depths)

    half = n * R // 2
    mine = pl.ds(pl.multiple_of(q * half, half), half)
    theirs = pl.ds(pl.multiple_of((1 - q) * half, half), half)
    lanes_mine = pl.ds(pl.multiple_of(q * LANES, LANES), LANES)
    lanes_theirs = pl.ds(pl.multiple_of((1 - q) * LANES, LANES), LANES)
    peer = {"col": 1 - q}

    def back(c):
        return f.at[pl.ds(c * (n * per) + me * per, per)]

    back_last = last.at[pl.ds(me * per, per)]

    def chunk(c, carry):
        at = pl.ds(c * per, per)
        arrived = z.at[at, pl.ds(0, n - 1)]
        pltpu.make_async_copy(arrived, arrived, recv1.at[c]).wait()
        own_copy(c).wait()

        line = tuple(jnp.concatenate([m[1, mine, :], m[1, theirs, :]], axis=0) for m in (mh, ml))
        for s in range(0, per, pair):
            i = c * per + s
            k = jnp.concatenate([z[i + e].reshape(n * R, LANES) for e in range(pair)], axis=1)
            out = dot3(line, split(react(k, rate, level)))
            for e in range(pair):
                part = out[:, e * LANES : (e + 1) * LANES]
                v[i + e, :, lanes_mine] = part[:half]
                w[i + e] = part[half:]
        to_peer = pltpu.make_async_remote_copy(
            src_ref=w.at[at],
            dst_ref=v.at[at, :, lanes_mine],
            send_sem=a_send.at[c],
            recv_sem=a_recv.at[c],
            device_id=peer,
            device_id_type=MESH,
        )
        to_peer.start()
        to_peer.wait()

        k = v[at].reshape(per * half, 2 * LANES)
        k = dot3(split(react(k, rate, level)), (mh[2], ml[2]))
        depth = tuple(
            jnp.concatenate([m[3, :, lanes_mine], m[3, :, lanes_theirs]], axis=1) for m in (mh, ml)
        )
        k = dot3(split(react(k, rate, level)), depth)
        t[at, mine, :] = k[:, :LANES].reshape(per, half, LANES)
        h[at] = k[:, LANES:].reshape(per, half, LANES)
        to_peer = pltpu.make_async_remote_copy(
            src_ref=h.at[at],
            dst_ref=t.at[at, mine, :],
            send_sem=b_send.at[c],
            recv_sem=b_recv.at[c],
            device_id=peer,
            device_id_type=MESH,
        )
        to_peer.start()
        to_peer.wait()

        line = (mh[4], ml[4])
        for s in range(0, per, pair):
            i = c * per + s
            k = jnp.concatenate([t[i + e] for e in range(pair)], axis=1)
            out = dot3(line, split(react(k, rate, level)))
            for e in range(pair):
                u[i + e] = out[:, e * LANES : (e + 1) * LANES].reshape(n, R, LANES)

        def send_back(target):
            def send_to(j, inner):
                d = lax.rem(me + j, n)
                pltpu.make_async_remote_copy(
                    src_ref=u.at[at, d],
                    dst_ref=target,
                    send_sem=send2,
                    recv_sem=recv2.at[c],
                    device_id={"row": d},
                    device_id_type=MESH,
                ).start()
                return inner

            lax.fori_loop(1, n, send_to, 0)
            pltpu.make_async_copy(u.at[at, me], target, own2.at[c]).start()

        @pl.when(c < C - 1)
        def _():
            send_back(back(c))

        @pl.when(c == C - 1)
        def _():
            send_back(back_last)

        return carry

    lax.fori_loop(0, C, chunk, 0)

    def wait_back(c, carry):
        arrived = f.at[pl.ds(c * (n * per), (n - 1) * per)]
        pltpu.make_async_copy(arrived, arrived, recv2.at[c]).wait()
        pltpu.make_async_copy(u.at[pl.ds(c * per, per), me], back(c), own2.at[c]).wait()
        return carry

    lax.fori_loop(0, C - 1, wait_back, 0)
    lead = ma[...]

    def o_copy(g):
        rows = pl.ds(g * group, group)
        return pltpu.make_async_copy(x.at[:, rows], o_hbm.at[:, rows], o_sem.at[g])

    for g in range(G):

        def begin(s, carry, g=g):
            r = g * group + s * cols
            store_columns(x, r, cols, terms(lead, f, r, cols, rate, level))
            return carry

        loop_columns(group // cols, x, begin)
        o_copy(g).start()
    for g in range(G):
        o_copy(g).wait()

    away = y.at[pl.ds(0, (n - 1) * L)]
    pltpu.make_async_copy(away, away, send1).wait()
    pltpu.make_async_copy(away, away, send2).wait()
    arrived = last.at[pl.ds(0, (n - 1) * per)]
    pltpu.make_async_copy(arrived, arrived, recv2.at[C - 1]).wait()
    pltpu.make_async_copy(u.at[pl.ds((C - 1) * per, per), me], back_last, own2.at[C - 1]).wait()


def terms(matrix, ref, r, cols, rate, level):
    hi, lo = split(react(load_columns(ref, r, cols, 0, ref.shape[0]), rate, level))
    k = jnp.concatenate([hi, lo, hi], axis=0)
    return jnp.dot(matrix, k, preferred_element_type=jnp.float32)


def last_kernel(species, rates, levels, matrix_ref, last_ref, sum_ref, o_ref):
    kind = species[0]
    rate, level = rates[kind], levels[kind]
    lines, R, lanes = o_ref.shape
    cols = 2 if R % 2 == 0 else 1
    matrix = matrix_ref[...]

    for s in range(R // cols):
        total = load_columns(sum_ref, s * cols, cols, 0, lines)
        total += terms(matrix, last_ref, s * cols, cols, rate, level)
        store_columns(o_ref, s * cols, cols, total)


def on_device(
    n,
    concentration,
    species,
    reaction_rates,
    levels,
    sweep_flags,
    explicit_line,
    inverse_line,
    explicit_depth,
    inverse_depth,
):
    lines, R, lanes = concentration.shape
    L = lines // n
    C = max(2, L // 16)
    G = max(1, R // 8)
    per = L // C
    half = n * R // 2
    f32, bf16 = jnp.float32, jnp.bfloat16

    c, source, e = np.meshgrid(np.arange(C), np.arange(n), np.arange(per), indexing="ij")
    held = (source * L + c * per + e).reshape(-1)
    early = (C - 1) * n * per
    picks = []
    for part in (held[:early], held[early:]):
        pick = np.zeros((lines, len(part)), np.float32)
        pick[part, np.arange(len(part))] = 1
        none = np.zeros_like(pick)
        picks.append(
            np.stack([np.concatenate(m, 1) for m in ((pick, pick, none), (none, none, pick))])
        )
    pick_a, pick_b = (jnp.asarray(p.astype(bf16)) for p in picks)

    any_spec = pl.BlockSpec(memory_space=pl.ANY)
    smem = pl.BlockSpec(memory_space=pltpu.SMEM)
    vmem = pl.BlockSpec(memory_space=pltpu.VMEM)
    dma = pltpu.SemaphoreType.DMA
    whole = jax.ShapeDtypeStruct(concentration.shape, f32)
    partial_sum, last, matrix = pl.pallas_call(
        functools.partial(kernel, n, L, R, C, G),
        out_shape=(
            whole,
            jax.ShapeDtypeStruct((n * per, R, lanes), f32),
            jax.ShapeDtypeStruct((lines, pick_b.shape[2]), bf16),
        ),
        in_specs=[smem] * 4 + [vmem] * 2 + [any_spec] * 5,
        out_specs=(any_spec, any_spec, vmem),
        scratch_shapes=[
            pltpu.VMEM((lines, R, lanes), f32),
            pltpu.VMEM((lines, R, lanes), f32),
            pltpu.VMEM((L, n, R, lanes), f32),
            pltpu.VMEM((L, half, lanes), f32),
            pltpu.VMEM((L, half, 2 * lanes), f32),
            pltpu.VMEM((L, half, lanes), f32),
            pltpu.VMEM((L, 2 * half, lanes), f32),
            pltpu.VMEM((L, n, R, lanes), f32),
            pltpu.VMEM((early, R, lanes), f32),
            pltpu.VMEM((5, lines, lines), bf16),
            pltpu.VMEM((5, lines, lines), bf16),
            pltpu.VMEM((lines, pick_a.shape[2]), bf16),
            pltpu.VMEM(explicit_depth.shape, f32),
            pltpu.VMEM(inverse_depth.shape, f32),
            pltpu.VMEM(pick_a.shape, bf16),
            pltpu.VMEM(pick_b.shape, bf16),
            dma((G,)),
            dma((C,)),
            dma((C,)),
            dma,
            dma((C,)),
            dma,
            dma((C,)),
            dma((C,)),
            dma((C,)),
            dma((C,)),
            dma((C,)),
            dma((G,)),
            dma((4,)),
        ],
        compiler_params=pltpu.CompilerParams(
            collective_id=0, has_side_effects=True, vmem_limit_bytes=58 << 20
        ),
    )(
        species, reaction_rates, levels, sweep_flags,
        explicit_line, inverse_line, explicit_depth, inverse_depth,
        pick_a, pick_b, concentration,
    )

    rows = R // G
    return pl.pallas_call(
        last_kernel,
        grid=(G,),
        out_shape=whole,
        in_specs=[
            smem,
            smem,
            smem,
            pl.BlockSpec(matrix.shape, lambda g: (0, 0)),
            pl.BlockSpec((n * per, rows, lanes), lambda g: (0, g, 0)),
            pl.BlockSpec((lines, rows, lanes), lambda g: (0, g, 0)),
        ],
        out_specs=pl.BlockSpec((lines, rows, lanes), lambda g: (0, g, 0)),
        compiler_params=pltpu.CompilerParams(vmem_limit_bytes=58 << 20),
    )(species, reaction_rates, levels, matrix, last, partial_sum)


def solution(mesh):
    in_specs = (P("groups", "row", "col"), P("groups"), P(), P(), P(), P(), P(), P(), P())
    out_specs = P("groups", "row", "col")
    return jax.shard_map(
        functools.partial(on_device, mesh.shape["row"]),
        mesh=mesh, in_specs=in_specs, out_specs=out_specs, check_vma=False,
    )
```
